32 devices in a mesh: gx: 8 (over z, x), gy: 4 (over y, core).
Axes of the slice: x: 2, y: 2, z: 4, core: 2. Of those that a mesh axis runs over, the one named last changes fastest.
Arguments:
- right_side: float32 [4096, 128], P(('gx', 'gy'))
- compress: float32 [4096, 128], P(('gx', 'gy')), may hold values from 0.5 to 8
- block_fill: int32 [4096], P(('gx', 'gy')), may hold values from 32 to 128, as said below
- pair_home: int32 [12288], P(('gx', 'gy')), may hold values from 0 to 4095, as said below
- pair_far: int32 [12288], P(('gx', 'gy')), may hold values from 0 to 4095, as said below
- pair_count: int32 [32], P(('gx', 'gy')), may hold values from 1 to 384, as said below
- weights: bfloat16 [12288, 128, 128], P(('gx', 'gy')), may hold values from 0 to 0.015625
Outputs:
- solution_field: float32 [4096, 128], P(('gx', 'gy'))
- residual: float32 [4096, 128], P(('gx', 'gy'))
The draws below stay inside these ranges and needn't reach their ends.
Inputs may be any that keep to these rules, and one draw needn't show every extreme that they name: `pair_home`: pair slot s names as first block a block of device s // 384, blocks of device d being d * 128 to d * 128 + 127, devices numbered gx major. `pair_far`: the second block belongs to the slot's device or to one of its eight neighbours on the periodic gx by gy grid of devices. `pair_count`: slots after a device's count are ignored; some devices hold 384. `block_fill`: slots after a block's fill are padding; some block holds 128.
All inputs are finite; a program needn't handle non-finite values.
Results may differ from the reference program's by a relative error of at most 0.015.
Values may be sent and summed in bfloat16 or wider, within the bound.
A program may use at most 64 MiB of HBM per device.

```python
import math
import jax
import jax.numpy as jnp
from jax import lax

TILE = 128
BLK_DEV = 128
PAIRS_DEV = 384
ITERS = 3
NBLK = 4096
NPAIR = 12288
N_GX = 8
N_GY = 4
DEVICES = 32


def draw_right_side(key, part):
    ramp = 1.0 + 2.0 * jnp.arange(NBLK, dtype=jnp.float32)[:, None] / max(NBLK - 1, 1)
    rough = jax.random.normal(key, (NBLK, TILE), jnp.float32)
    return jnp.clip(rough, -4.0, 4.0) * ramp


def draw_block_fill(key, part):
    fill = jax.random.randint(jax.random.fold_in(key, 11), (NBLK,), TILE // 4, TILE + 1)
    where = jax.random.randint(jax.random.fold_in(key, 12), (), 0, NBLK)
    return fill.at[where].set(TILE).astype(jnp.int32)


def draw_pair_home(key, part):
    device = jnp.arange(NPAIR, dtype=jnp.int32) // PAIRS_DEV
    inside = jax.random.randint(jax.random.fold_in(key, 21), (NPAIR,), 0, BLK_DEV)
    return (device * BLK_DEV + inside).astype(jnp.int32)


def draw_pair_far(key, part):
    device = jnp.arange(NPAIR, dtype=jnp.int32) // PAIRS_DEV
    first_index = device // N_GY
    second_index = device % N_GY
    step_first = jax.random.randint(jax.random.fold_in(key, 31), (NPAIR,), -1, 2)
    step_second = jax.random.randint(jax.random.fold_in(key, 32), (NPAIR,), -1, 2)
    target = (first_index + step_first) % N_GX * N_GY + (second_index + step_second) % N_GY
    inside = jax.random.randint(jax.random.fold_in(key, 33), (NPAIR,), 0, BLK_DEV)
    return (target * BLK_DEV + inside).astype(jnp.int32)


def draw_pair_count(key, part):
    device = jnp.arange(DEVICES, dtype=jnp.int32)
    band = jax.random.randint(jax.random.fold_in(key, 41), (), 0, N_GX)
    heavy = (device // N_GY - band) % N_GX < 2
    light = jax.random.randint(jax.random.fold_in(key, 42), (DEVICES,), PAIRS_DEV // 8, PAIRS_DEV // 3 + 1)
    return jnp.where(heavy, PAIRS_DEV, light).astype(jnp.int32)


def steps_of(key, shape, split, smallest, largest):
    def one(position, blocks):
        draws = jax.random.uniform(jax.random.fold_in(jax.random.fold_in(key, 6), position), (blocks,), jnp.float32, smallest / len(split), largest / len(split))
        return jnp.repeat(jnp.exp(draws), shape[position] // blocks).reshape((-1,) + (1,) * (len(shape) - position - 1))

    loudness = one(*split[0])
    for cut in split[1:]:
        loudness = loudness * one(*cut)
    return loudness


def setup_inputs(seed: int = 0) -> dict:
    keys = jax.random.split(jax.random.key(seed), 8)
    return {
        "right_side": draw_right_side(jax.random.fold_in(keys[7], 71), 0),
        "compress": jnp.clip(jnp.exp(math.log(8.0) - 2.7725887 * jax.random.uniform(keys[1], (NBLK, TILE), jnp.float32) ** steps_of(keys[1], (NBLK, TILE), ((0, 32),), -0.2, 0.2)), 0.5, 8.0),
        "block_fill": draw_block_fill(jax.random.fold_in(keys[7], 71), 0),
        "pair_home": draw_pair_home(jax.random.fold_in(keys[7], 71), 0),
        "pair_far": draw_pair_far(jax.random.fold_in(keys[7], 71), 0),
        "pair_count": draw_pair_count(jax.random.fold_in(keys[7], 71), 0),
        "weights": jnp.clip(0.015625 * jax.random.uniform(keys[6], (NPAIR, TILE, TILE), jnp.float32) ** steps_of(keys[6], (NPAIR, TILE, TILE), ((0, 32),), -0.2, 0.2), 0.0, 0.015625).astype(jnp.bfloat16),
    }


def apply_operator(field, compress, live, weights, pair_home, pair_far, slot_live):
    quant = (live * field).astype(jnp.bfloat16).astype(jnp.float32)
    stacks = (weights.reshape(DEVICES, PAIRS_DEV, TILE, TILE), pair_home.reshape(DEVICES, PAIRS_DEV),
              pair_far.reshape(DEVICES, PAIRS_DEV), slot_live.reshape(DEVICES, PAIRS_DEV))

    def one_device(totals, pieces):
        tiles, homes, fars, keep = pieces
        tiles = tiles.astype(jnp.float32)
        row_sum = jnp.sum(tiles, axis=2)
        col_sum = jnp.sum(tiles, axis=1)
        first = quant[homes]
        second = quant[fars]
        toward = jnp.einsum("pij,pj->pi", tiles, second, precision=lax.Precision.HIGHEST)
        backward = jnp.einsum("pij,pi->pj", tiles, first, precision=lax.Precision.HIGHEST)
        term_home = (row_sum * first - toward) * keep[:, None]
        term_far = (col_sum * second - backward) * keep[:, None]
        totals = totals.at[homes].add(term_home).at[fars].add(term_far)
        return totals, None

    pairs_sum, _ = lax.scan(one_device, jnp.zeros((NBLK, TILE), jnp.float32), stacks)
    return compress * field + live * pairs_sum


def reference(right_side, compress, block_fill, pair_home, pair_far, pair_count, weights):
    live = (jnp.arange(TILE, dtype=jnp.int32)[None, :] < block_fill[:, None]).astype(jnp.float32)
    slot_index = jnp.arange(NPAIR, dtype=jnp.int32)
    slot_live = ((slot_index % PAIRS_DEV) < pair_count[slot_index // PAIRS_DEV]).astype(jnp.float32)
    solution_field = jnp.zeros_like(right_side)
    residual = right_side
    direction = right_side
    norm_now = jnp.sum(residual * residual)
    for step in range(ITERS):
        image = apply_operator(direction, compress, live, weights, pair_home, pair_far, slot_live)
        alpha = norm_now / jnp.sum(direction * image)
        solution_field = solution_field + alpha * direction
        residual = residual - alpha * image
        norm_next = jnp.sum(residual * residual)
        direction = residual + (norm_next / norm_now) * direction
        norm_now = norm_next
    return solution_field, residual
```

```python
import functools

import jax
import jax.numpy as jnp
from jax import lax
from jax.experimental import pallas as pl
from jax.experimental.pallas import tpu as pltpu
from jax.sharding import PartitionSpec as P

ITERS = 3
GROUP = 16
UNROLL = 6
MESH = pl.DeviceIdType.MESH
F32 = jnp.float32
BF16 = jnp.bfloat16


def matmul(a, b):
    return jnp.dot(a, b, preferred_element_type=F32)


def halves(value):
    high = value.astype(BF16)
    return high, (value - high.astype(F32)).astype(BF16)


def kernel(
    sizes,
    right_hbm,
    compress_hbm,
    fill_hbm,
    home_hbm,
    far_hbm,
    count_ref,
    weights_hbm,
    x_ref,
    r_ref,
    right_ref,
    compress_ref,
    fill_ref,
    home_ref,
    far_ref,
    wv,
    wt,
    onehot_home_t,
    onehot_home,
    onehot_far_t,
    onehot_far,
    mask,
    live,
    degree,
    gathered,
    rows_out,
    rows_sum,
    local,
    w_now,
    s_now,
    d_now,
    onward,
    nearby,
    give,
    take,
    far_deg,
    give_deg,
    take_deg,
    red_y,
    red_x,
    load_sem,
    in_sem,
    halo_send,
    halo_recv,
    ret_send,
    ret_recv,
    deg_send,
    deg_recv,
    ry_send,
    ry_recv,
    rx_send,
    rx_recv,
):
    n_x, n_y, chunks = sizes
    blocks, tile = right_hbm.shape
    npairs = weights_hbm.shape[0]
    groups = npairs // GROUP
    per_chunk = npairs // chunks
    my_x = lax.axis_index("gx")
    my_y = lax.axis_index("gy")

    def at(dx, dy):
        return (lax.rem(my_x + dx + n_x, n_x), lax.rem(my_y + dy + n_y, n_y))

    friends = {(dx % n_x, dy % n_y) for dx in (-1, 0, 1) for dy in (-1, 0, 1)}
    friends |= {(0, dy) for dy in range(n_y)} | {(dx, 0) for dx in range(n_x)}
    friends = sorted(friends - {(0, 0)})
    barrier = pltpu.get_barrier_semaphore()
    for dx, dy in friends:
        pl.semaphore_signal(barrier, inc=1, device_id=at(dx, dy), device_id_type=MESH)

    inputs = [
        pltpu.make_async_copy(src, dst, in_sem.at[i])
        for i, (src, dst) in enumerate(
            (
                (fill_hbm, fill_ref),
                (right_hbm, right_ref),
                (home_hbm, home_ref),
                (far_hbm, far_ref),
                (compress_hbm, compress_ref),
            )
        )
    ]
    for copy in inputs:
        copy.start()
    loads = [
        pltpu.make_async_copy(
            weights_hbm.at[pl.ds(i * per_chunk, per_chunk)],
            wv.at[pl.ds(i * per_chunk, per_chunk)],
            load_sem.at[i],
        )
        for i in range(chunks)
    ]
    for load in loads:
        load.start()

    longer = 2 * lax.rem(my_x, 2) - 1
    order = [(longer, dy) for dy in (1, -1, 0)] + [(-longer, dy) for dy in (1, -1, 0)]
    order += [(0, 1), (0, -1)]
    around = [((dx + 1) * 3 + dy + 1, dx, dy) for dx, dy in order]

    def send(to, src, dst, ssem, rsem):
        return pltpu.make_async_remote_copy(
            src_ref=src,
            dst_ref=dst,
            send_sem=ssem,
            recv_sem=rsem,
            device_id=at(to[1], to[2]),
            device_id_type=MESH,
        )

    def halo(k):
        return [
            send(to, nearby.at[k, 4], nearby.at[k, 8 - to[0]], halo_send.at[k, to[0]], halo_recv.at[k, 8 - to[0]])
            for to in around
        ]

    def returns(k):
        return [
            send(to, give.at[k, to[0]], take.at[k, 8 - to[0]], ret_send.at[k, to[0]], ret_recv.at[k, 8 - to[0]])
            for to in around
        ]

    def degrees():
        return [
            send(to, give_deg.at[to[0]], take_deg.at[8 - to[0]], deg_send.at[to[0]], deg_recv.at[8 - to[0]])
            for to in around
        ]

    for copy in inputs[:2]:
        copy.wait()
    fill = jnp.broadcast_to(fill_ref[...].astype(F32), (tile, blocks)).T
    live_now = (lax.broadcasted_iota(jnp.int32, (blocks, tile), 1).astype(F32) < fill).astype(F32)
    live[...] = live_now
    nearby[0, 4] = (live_now * right_ref[...]).astype(BF16)

    pl.semaphore_wait(barrier, len(friends))
    for copy in halo(0):
        copy.start()

    for copy in inputs[2:]:
        copy.wait()
    keep = lax.broadcasted_iota(jnp.int32, (1, npairs), 1) < count_ref[0]
    home_row = jnp.broadcast_to(jnp.where(keep, home_ref[...], -1), (blocks, npairs))
    far_row = jnp.broadcast_to(jnp.where(keep, far_ref[...], -1), (blocks, npairs))
    which = lax.broadcasted_iota(jnp.int32, (blocks, npairs), 0)
    pick = jnp.where(which + (my_x * n_y + my_y) * blocks == home_row, 1.0, 0.0)
    onehot_home_t[...] = pick.astype(BF16)
    onehot_home[...] = pick.T.astype(BF16)
    for n in range(9):
        far_x, far_y = at(n // 3 - 1, n % 3 - 1)
        pick = jnp.where(which + (far_x * n_y + far_y) * blocks == far_row, 1.0, 0.0)
        onehot_far_t[n * blocks : (n + 1) * blocks, :] = pick.astype(BF16)
        onehot_far[:, n * blocks : (n + 1) * blocks] = pick.T.astype(BF16)
    for p in range(GROUP):
        own = lax.broadcasted_iota(jnp.int32, (GROUP, tile), 0) == p
        mask[:, p * tile : (p + 1) * tile] = jnp.where(own, 1.0, 0.0).astype(BF16)

    def rows(g):
        return pl.ds(pl.multiple_of(g * GROUP, GROUP), GROUP)

    def group_products(first, turn, held, g, carry):
        x = gathered[rows(g), :]
        spread = mask[...]
        lhs = jnp.concatenate([x] * GROUP, axis=1) * spread
        if first:
            lhs = jnp.concatenate([lhs, spread], axis=0)
        if turn:
            rhs = jnp.concatenate([held[g * GROUP + p] for p in range(GROUP)], axis=1)
            out = lax.dot_general(lhs, rhs, (((1,), (1,)), ((), ())), preferred_element_type=F32)
        else:
            out = matmul(lhs, held[pl.ds(g * GROUP, GROUP)].reshape(GROUP * tile, tile))
        rows_out[rows(g), :] = out[:GROUP].astype(BF16)
        if first:
            rows_sum[rows(g), :] = out[GROUP:]
        return carry

    def products(first, turn, held, start, stop, unroll=UNROLL):
        lax.fori_loop(start, stop, functools.partial(group_products, first, turn, held), 0, unroll=unroll)

    def turn_tiles(g, carry):
        for p in range(GROUP):
            wt[g * GROUP + p] = wv[g * GROUP + p].T
        return carry

    def operate(k, field, during=None, late=None):
        first = k == 0
        gathered[...] = matmul(onehot_home[...], nearby[k, 4]).astype(BF16)
        if first:
            per = groups // chunks
            for i in range(chunks):
                loads[i].wait()
                products(True, False, wv, i * per, (i + 1) * per)
            high, low = halves(rows_sum[...])
            for n in range(9):
                select = onehot_far_t[n * blocks : (n + 1) * blocks, :]
                far_deg[n] = matmul(select, high) + matmul(select, low)
                give_deg[n] = far_deg[n].astype(BF16)
            for copy in halo(k):
                copy.wait_recv()
        else:
            products(False, False, wv, 0, groups)
        terms = rows_out[...]
        for n in (0, 1, 2, 6, 7, 8, 3, 5, 4):
            total = matmul(onehot_far_t[n * blocks : (n + 1) * blocks, :], terms)
            if first and n != 4:
                total -= far_deg[n] * nearby[k, n].astype(F32)
            if n == 4:
                local[...] = total
            else:
                give[k, n] = total.astype(BF16)
        for copy in returns(k):
            copy.start()
        if first:
            for copy in degrees():
                copy.start()
        if during is not None:
            during()
        if k == 1:
            lax.fori_loop(groups // 2, groups, turn_tiles, 0, unroll=2)
        if not first:
            for copy in halo(k):
                copy.wait_recv()
        gathered[...] = matmul(onehot_far[...], nearby[k].reshape(9 * blocks, tile)).astype(BF16)
        if late is not None:
            across = jnp.sum(terms.astype(F32) * gathered[...].astype(F32), axis=0, keepdims=True)
            own = nearby[k, 4].astype(F32)
            within = jnp.sum(
                compress_ref[...] * field * field + degree[...] * own * own, axis=0, keepdims=True
            )
            late(within - 2.0 * across)
        if first:
            products(True, True, wv, 0, groups, 3)
            high, low = halves(rows_sum[...])
            select = onehot_home_t[...]
            degree[...] = far_deg[4] + matmul(select, high) + matmul(select, low)
        else:
            products(False, False, wt, 0, groups)
        total = local[...] + matmul(onehot_home_t[...], rows_out[...])
        if late is not None:
            sums_middle(k)
        if first:
            lax.fori_loop(0, groups // 2, turn_tiles, 0, unroll=2)
        if k == 1:
            for copy in degrees():
                copy.wait_recv()
            for n in (0, 1, 2, 3, 5, 6, 7, 8):
                degree[...] += take_deg[n].astype(F32)
        for copy in returns(k):
            copy.wait_recv()
        for n in (0, 1, 2, 3, 5, 6, 7, 8):
            total += take[k, n].astype(F32)
        pairs = degree[...] * nearby[k, 4].astype(F32) - total
        return compress_ref[...] * field + live[...] * pairs

    def sum_y(k):
        return [
            pltpu.make_async_remote_copy(
                src_ref=red_y.at[k, my_y],
                dst_ref=red_y.at[k, my_y],
                send_sem=ry_send.at[k, d],
                recv_sem=ry_recv.at[k, n_y - d],
                device_id=at(0, d),
                device_id_type=MESH,
            )
            for d in range(1, n_y)
        ]

    def sum_x(k):
        return [
            pltpu.make_async_remote_copy(
                src_ref=red_x.at[k, my_x],
                dst_ref=red_x.at[k, my_x],
                send_sem=rx_send.at[k, d],
                recv_sem=rx_recv.at[k, n_x - d],
                device_id=at(d, 0),
                device_id_type=MESH,
            )
            for d in range(1, n_x)
        ]

    def column(value):
        return jnp.sum(value, axis=0, keepdims=True)

    def sums_start(k, terms):
        which_row = lax.broadcasted_iota(jnp.int32, (8, tile), 0)
        packed = jnp.zeros((8, tile), F32)
        for i, term in enumerate(terms):
            packed = jnp.where(which_row == i, term, packed)
        red_y[k, my_y] = packed
        for copy in sum_y(k):
            copy.start()

    def sums_middle(k):
        for copy in sum_y(k):
            copy.wait_recv()
        red_x[k, my_x] = jnp.sum(red_y[k], axis=0)
        for copy in sum_x(k):
            copy.start()

    def sums_end(k):
        for copy in sum_x(k):
            copy.wait_recv()
        totals = jnp.sum(jnp.sum(red_x[k], axis=0), axis=1, keepdims=True)
        return [totals[i : i + 1, :] for i in range(8)]

    residual = right_ref[...]
    image = operate(0, residual)
    r_ref[...] = residual
    w_now[...] = image
    sums_start(0, (column(residual * residual), column(residual * image)))
    s_now[...] = image
    nearby[1, 4] = (live[...] * image).astype(BF16)
    for copy in halo(1):
        copy.start()
    onward[...] = operate(1, image, lambda: sums_middle(0))
    norm_now, product = sums_end(0)[:2]
    alpha = norm_now / product
    x_ref[...] = alpha * residual
    d_now[...] = residual
    residual = residual - alpha * s_now[...]
    image = image - alpha * onward[...]
    for k in range(1, ITERS - 1):
        final = k + 2 == ITERS
        r_ref[...] = residual
        w_now[...] = image
        sums_start(k, (column(residual * residual), column(residual * image)))
        nearby[k + 1, 4] = (live[...] * image).astype(BF16)
        for copy in halo(k + 1):
            copy.start()
        coefficients = []

        def advance():
            norm_next, product = sums_end(k)[:2]
            ratio = norm_next / norm_now
            alpha_next = norm_next / (product - ratio * norm_next / alpha)
            coefficients.extend((norm_next, ratio, alpha_next))
            d_now[...] = r_ref[...] + ratio * d_now[...]
            s_now[...] = w_now[...] + ratio * s_now[...]
            x_ref[...] += alpha_next * d_now[...]
            r_ref[...] -= alpha_next * s_now[...]

        def early(energy):
            advance()
            r_next, w, q = r_ref[...], w_now[...], onward[...]
            sums_start(
                k + 1,
                (column(r_next * r_next), column(r_next * w), column(r_next * q), column(w * w), column(q * w), energy),
            )

        if final:
            further = operate(k + 1, image, lambda: sums_middle(k), early)
        else:
            further = operate(k + 1, image, lambda: sums_middle(k))
            advance()
        norm_now, ratio, alpha = coefficients
        onward[...] = further + ratio * onward[...]
        residual = r_ref[...]
        image = w_now[...] - alpha * onward[...]
    norm_last, r_w, r_q, w_w, q_w, energy = sums_end(ITERS - 1)[:6]
    product = r_w - alpha * (w_w - alpha * (energy + ratio * q_w)) - alpha * ratio * r_q
    ratio = norm_last / norm_now
    alpha = norm_last / (product - ratio * norm_last / alpha)
    x_ref[...] += alpha * (residual + ratio * d_now[...])
    r_ref[...] = residual - alpha * (image + ratio * s_now[...])

    for k in range(ITERS):
        for copy in halo(k) + returns(k) + sum_y(k) + sum_x(k):
            copy.wait_send()
    for copy in degrees():
        copy.wait_send()


def on_device(mesh_sizes, right_side, compress, block_fill, pair_home, pair_far, pair_count, weights):
    n_x, n_y = mesh_sizes
    blocks, tile = right_side.shape
    npairs = weights.shape[0]
    chunks = 4
    dma = pltpu.SemaphoreType.DMA
    vmem = pl.BlockSpec(memory_space=pltpu.VMEM)
    out = jax.ShapeDtypeStruct((blocks, tile), F32)
    return pl.pallas_call(
        functools.partial(kernel, (n_x, n_y, chunks)),
        out_shape=(out, out),
        in_specs=[pl.BlockSpec(memory_space=pl.ANY)] * 5
        + [pl.BlockSpec(memory_space=pltpu.SMEM), pl.BlockSpec(memory_space=pl.ANY)],
        out_specs=(vmem, vmem),
        scratch_shapes=[
            pltpu.VMEM((blocks, tile), F32),
            pltpu.VMEM((blocks, tile), F32),
            pltpu.VMEM((1, blocks), jnp.int32),
            pltpu.VMEM((1, npairs), jnp.int32),
            pltpu.VMEM((1, npairs), jnp.int32),
            pltpu.VMEM((npairs, tile, tile), BF16),
            pltpu.VMEM((npairs, tile, tile), BF16),
            pltpu.VMEM((blocks, npairs), BF16),
            pltpu.VMEM((npairs, blocks), BF16),
            pltpu.VMEM((9 * blocks, npairs), BF16),
            pltpu.VMEM((npairs, 9 * blocks), BF16),
            pltpu.VMEM((GROUP, GROUP * tile), BF16),
            pltpu.VMEM((blocks, tile), F32),
            pltpu.VMEM((blocks, tile), F32),
            pltpu.VMEM((npairs, tile), BF16),
            pltpu.VMEM((npairs, tile), BF16),
            pltpu.VMEM((npairs, tile), F32),
            pltpu.VMEM((blocks, tile), F32),
            pltpu.VMEM((blocks, tile), F32),
            pltpu.VMEM((blocks, tile), F32),
            pltpu.VMEM((blocks, tile), F32),
            pltpu.VMEM((blocks, tile), F32),
            pltpu.VMEM((ITERS, 9, blocks, tile), BF16),
            pltpu.VMEM((ITERS, 9, blocks, tile), BF16),
            pltpu.VMEM((ITERS, 9, blocks, tile), BF16),
            pltpu.VMEM((9, blocks, tile), F32),
            pltpu.VMEM((9, blocks, tile), BF16),
            pltpu.VMEM((9, blocks, tile), BF16),
            pltpu.VMEM((ITERS, n_y, 8, tile), F32),
            pltpu.VMEM((ITERS, n_x, 8, tile), F32),
            dma((chunks,)),
            dma((5,)),
            dma((ITERS, 9)),
            dma((ITERS, 9)),
            dma((ITERS, 9)),
            dma((ITERS, 9)),
            dma((9,)),
            dma((9,)),
            dma((ITERS, n_y)),
            dma((ITERS, n_y)),
            dma((ITERS, n_x)),
            dma((ITERS, n_x)),
        ],
        compiler_params=pltpu.CompilerParams(
            collective_id=0, has_side_effects=True, vmem_limit_bytes=56 * 1024 * 1024
        ),
    )(right_side, compress, block_fill[None], pair_home[None], pair_far[None], pair_count, weights)


def solution(mesh):
    return jax.shard_map(
        functools.partial(on_device, (mesh.shape["gx"], mesh.shape["gy"])),
        mesh=mesh,
        in_specs=(
            P(("gx", "gy"), None),
            P(("gx", "gy"), None),
            P(("gx", "gy")),
            P(("gx", "gy")),
            P(("gx", "gy")),
            P(("gx", "gy")),
            P(("gx", "gy"), None, None),
        ),
        out_specs=(P(("gx", "gy"), None), P(("gx", "gy"), None)),
        check_vma=False,
    )
```

```python
import functools

import jax
import jax.numpy as jnp
from jax import lax
from jax.experimental import pallas as pl
from jax.experimental.pallas import tpu as pltpu
from jax.sharding import PartitionSpec as P

ITERS = 3
GROUP = 16
UNROLL = 6
MESH = pl.DeviceIdType.MESH
F32 = jnp.float32
BF16 = jnp.bfloat16


def matmul(a, b):
    return jnp.dot(a, b, preferred_element_type=F32)


def halves(value):
    high = value.astype(BF16)
    return high, (value - high.astype(F32)).astype(BF16)


def kernel(
    sizes,
    right_hbm,
    compress_hbm,
    fill_hbm,
    home_hbm,
    far_hbm,
    count_ref,
    weights_hbm,
    x_ref,
    r_ref,
    right_ref,
    compress_ref,
    fill_ref,
    home_ref,
    far_ref,
    wv,
    wt,
    onehot_home_t,
    onehot_home,
    onehot_far_t,
    onehot_far,
    mask,
    live,
    degree,
    gathered,
    rows_out,
    rows_sum,
    local,
    w_now,
    s_now,
    d_now,
    onward,
    nearby,
    give,
    take,
    far_deg,
    give_deg,
    take_deg,
    red_y,
    red_x,
    load_sem,
    in_sem,
    halo_send,
    halo_recv,
    ret_send,
    ret_recv,
    deg_send,
    deg_recv,
    ry_send,
    ry_recv,
    rx_send,
    rx_recv,
):
    n_x, n_y, chunks = sizes
    blocks, tile = right_hbm.shape
    npairs = weights_hbm.shape[0]
    groups = npairs // GROUP
    per_chunk = npairs // chunks
    my_x = lax.axis_index("gx")
    my_y = lax.axis_index("gy")

    def at(dx, dy):
        return (lax.rem(my_x + dx + n_x, n_x), lax.rem(my_y + dy + n_y, n_y))

    friends = {(dx % n_x, dy % n_y) for dx in (-1, 0, 1) for dy in (-1, 0, 1)}
    friends |= {(0, dy) for dy in range(n_y)} | {(dx, 0) for dx in range(n_x)}
    friends = sorted(friends - {(0, 0)})
    barrier = pltpu.get_barrier_semaphore()
    for dx, dy in friends:
        pl.semaphore_signal(barrier, inc=1, device_id=at(dx, dy), device_id_type=MESH)

    inputs = [
        pltpu.make_async_copy(src, dst, in_sem.at[i])
        for i, (src, dst) in enumerate(
            (
                (fill_hbm, fill_ref.at[0]),
                (right_hbm, right_ref),
                (home_hbm, home_ref.at[0]),
                (far_hbm, far_ref.at[0]),
                (compress_hbm, compress_ref),
            )
        )
    ]
    for copy in inputs:
        copy.start()
    loads = [
        pltpu.make_async_copy(
            weights_hbm.at[pl.ds(i * per_chunk, per_chunk)],
            wv.at[pl.ds(i * per_chunk, per_chunk)],
            load_sem.at[i],
        )
        for i in range(chunks)
    ]
    loads[0].start()

    longer = 2 * lax.rem(my_x, 2) - 1
    order = [(longer, dy) for dy in (1, -1, 0)] + [(-longer, dy) for dy in (1, -1, 0)]
    order += [(0, 1), (0, -1)]
    around = [((dx + 1) * 3 + dy + 1, dx, dy) for dx, dy in order]

    def send(to, src, dst, ssem, rsem):
        return pltpu.make_async_remote_copy(
            src_ref=src,
            dst_ref=dst,
            send_sem=ssem,
            recv_sem=rsem,
            device_id=at(to[1], to[2]),
            device_id_type=MESH,
        )

    def place(dx, dy):
        return (dx + 1) * 3 + dy + 1

    def halo(k):
        return [
            send((n, dx, dy), nearby.at[k, 4], nearby.at[k, 8 - n], halo_send.at[k, n], halo_recv.at[k, 8 - n])
            for n, dx, dy in ((place(dx, dy), dx, dy) for dx, dy in ((longer, 0), (-longer, 0), (0, 1), (0, -1)))
        ]

    def relay(k, dx):
        held = place(dx, 0)
        return [
            send(
                (0, 0, dy),
                nearby.at[k, held],
                nearby.at[k, place(dx, -dy)],
                halo_send.at[k, place(dx, dy)],
                halo_recv.at[k, place(dx, -dy)],
            )
            for dy in (1, -1)
        ]

    def halo_pass_on(k):
        for dx in (-longer, longer):
            arrived(k, place(dx, 0)).wait_recv()
            for copy in relay(k, dx):
                copy.start()

    def halo_finish(k):
        for n in (0, 2, 6, 8, 3, 5):
            arrived(k, n).wait_recv()

    def arrived(k, n):
        return send((0, 0, 1), nearby.at[k, 4], nearby.at[k, n], halo_send.at[k, 4], halo_recv.at[k, n])

    def returns(k):
        return [
            send(to, give.at[k, to[0]], take.at[k, 8 - to[0]], ret_send.at[k, to[0]], ret_recv.at[k, 8 - to[0]])
            for to in around
        ]

    def degrees_y():
        return [
            send(
                (0, 0, dy),
                give_deg.at[place(dx, dy)],
                take_deg.at[place(dx, -dy)],
                deg_send.at[place(dx, dy)],
                deg_recv.at[place(dx, -dy)],
            )
            for dx in (1, -1, 0)
            for dy in (1, -1)
        ]

    def degrees_x():
        return [
            send(
                (0, dx, 0),
                give_deg.at[place(dx, 0)],
                take_deg.at[place(-dx, 0)],
                deg_send.at[place(dx, 0)],
                deg_recv.at[place(-dx, 0)],
            )
            for dx in (1, -1)
        ]

    for copy in inputs[:4]:
        copy.wait()
    for load in loads[1:]:
        load.start()
    fill = jnp.broadcast_to(fill_ref[...].astype(F32), (tile, blocks)).T
    live_now = (lax.broadcasted_iota(jnp.int32, (blocks, tile), 1).astype(F32) < fill).astype(F32)
    live[...] = live_now
    nearby[0, 4] = (live_now * right_ref[...]).astype(BF16)

    pl.semaphore_wait(barrier, len(friends))
    for copy in halo(0):
        copy.start()

    keep = lax.broadcasted_iota(jnp.int32, (1, npairs), 1) < count_ref[0]
    home_row = jnp.broadcast_to(jnp.where(keep, home_ref[...], -1), (blocks, npairs))
    far_row = jnp.broadcast_to(jnp.where(keep, far_ref[...], -1), (blocks, npairs))
    which = lax.broadcasted_iota(jnp.int32, (blocks, npairs), 0)
    pick = jnp.where(which + (my_x * n_y + my_y) * blocks == home_row, 1.0, 0.0)
    onehot_home_t[...] = pick.astype(BF16)
    onehot_home[...] = pick.T.astype(BF16)
    for n in range(9):
        far_x, far_y = at(n // 3 - 1, n % 3 - 1)
        pick = jnp.where(which + (far_x * n_y + far_y) * blocks == far_row, 1.0, 0.0)
        onehot_far_t[n * blocks : (n + 1) * blocks, :] = pick.astype(BF16)
        onehot_far[:, n * blocks : (n + 1) * blocks] = pick.T.astype(BF16)
    for p in range(GROUP):
        own = lax.broadcasted_iota(jnp.int32, (GROUP, tile), 0) == p
        mask[:, p * tile : (p + 1) * tile] = jnp.where(own, 1.0, 0.0).astype(BF16)

    def rows(g):
        return pl.ds(pl.multiple_of(g * GROUP, GROUP), GROUP)

    def group_products(first, turn, held, g, carry):
        x = gathered[rows(g), :]
        spread = mask[...]
        lhs = jnp.concatenate([x] * GROUP, axis=1) * spread
        if first:
            lhs = jnp.concatenate([lhs, spread], axis=0)
        if turn:
            rhs = jnp.concatenate([held[g * GROUP + p] for p in range(GROUP)], axis=1)
            out = lax.dot_general(lhs, rhs, (((1,), (1,)), ((), ())), preferred_element_type=F32)
        else:
            out = matmul(lhs, held[pl.ds(g * GROUP, GROUP)].reshape(GROUP * tile, tile))
        rows_out[rows(g), :] = out[:GROUP].astype(BF16)
        if first:
            rows_sum[rows(g), :] = out[GROUP:]
        return carry

    def products(first, turn, held, start, stop, unroll=UNROLL):
        lax.fori_loop(start, stop, functools.partial(group_products, first, turn, held), 0, unroll=unroll)

    def turn_tiles(g, carry):
        for p in range(GROUP):
            wt[g * GROUP + p] = wv[g * GROUP + p].T
        return carry

    def operate(k, field, during=None, late=None):
        first = k == 0
        gathered[...] = matmul(onehot_home[...], nearby[k, 4]).astype(BF16)
        if first:
            per = groups // chunks
            for i in range(chunks):
                loads[i].wait()
                products(True, False, wv, i * per, (i + 1) * per)
            halo_pass_on(k)
            high, low = halves(rows_sum[...])
            for n in range(9):
                select = onehot_far_t[n * blocks : (n + 1) * blocks, :]
                far_deg[n] = matmul(select, high) + matmul(select, low)
                if n % 3 != 1:
                    give_deg[n] = far_deg[n].astype(BF16)
            lax.fori_loop(0, groups // 2, turn_tiles, 0, unroll=2)
            halo_finish(k)
        else:
            products(False, False, wv, 0, groups)
        if during is not None:
            during()
        terms = rows_out[...]
        for n in (0, 1, 2, 6, 7, 8, 3, 5, 4):
            total = matmul(onehot_far_t[n * blocks : (n + 1) * blocks, :], terms)
            if first and n != 4:
                total -= far_deg[n] * nearby[k, n].astype(F32)
            if n == 4:
                local[...] = total
            else:
                give[k, n] = total.astype(BF16)
        outgoing = returns(k)
        for copy in outgoing[:6]:
            copy.start()
        if not first:
            halo_pass_on(k)
        for copy in outgoing[6:]:
            copy.start()
        if first:
            for copy in degrees_y():
                copy.start()
        if k == 1:
            lax.fori_loop(groups // 2, groups, turn_tiles, 0, unroll=2)
        if not first:
            halo_finish(k)
        gathered[...] = matmul(onehot_far[...], nearby[k].reshape(9 * blocks, tile)).astype(BF16)
        if late is not None:
            across = jnp.sum(terms.astype(F32) * gathered[...].astype(F32), axis=0, keepdims=True)
            own = nearby[k, 4].astype(F32)
            within = jnp.sum(
                compress_ref[...] * field * field + degree[...] * own * own, axis=0, keepdims=True
            )
            late(within - 2.0 * across)
        if first:
            products(True, False, wt, 0, groups // 2)
            products(True, True, wv, groups // 2, groups, 3)
            high, low = halves(rows_sum[...])
            select = onehot_home_t[...]
            degree[...] = far_deg[4] + matmul(select, high) + matmul(select, low)
            for copy in degrees_y():
                copy.wait_recv()
            for dx in (1, -1):
                both = take_deg[place(dx, 1)].astype(F32) + take_deg[place(dx, -1)].astype(F32)
                give_deg[place(dx, 0)] = (far_deg[place(dx, 0)] + both).astype(BF16)
            for copy in degrees_x():
                copy.start()
        elif late is None:
            products(False, False, wt, 0, groups)
        else:
            products(False, False, wt, 0, groups * 3 // 4)
            sums_middle(k)
            products(False, False, wt, groups * 3 // 4, groups)
        total = local[...] + matmul(onehot_home_t[...], rows_out[...])
        if first:
            inputs[4].wait()
        if k == 1:
            for copy in degrees_x():
                copy.wait_recv()
            for n in (1, 3, 5, 7):
                degree[...] += take_deg[n].astype(F32)
        for copy in returns(k):
            copy.wait_recv()
        for n in (0, 1, 2, 3, 5, 6, 7, 8):
            total += take[k, n].astype(F32)
        pairs = degree[...] * nearby[k, 4].astype(F32) - total
        return compress_ref[...] * field + live[...] * pairs

    def sum_y(k):
        return [
            pltpu.make_async_remote_copy(
                src_ref=red_y.at[k, my_y],
                dst_ref=red_y.at[k, my_y],
                send_sem=ry_send.at[k, d],
                recv_sem=ry_recv.at[k, n_y - d],
                device_id=at(0, d),
                device_id_type=MESH,
            )
            for d in range(1, n_y)
        ]

    def sum_x(k):
        return [
            pltpu.make_async_remote_copy(
                src_ref=red_x.at[k, my_x],
                dst_ref=red_x.at[k, my_x],
                send_sem=rx_send.at[k, d],
                recv_sem=rx_recv.at[k, n_x - d],
                device_id=at(d, 0),
                device_id_type=MESH,
            )
            for d in range(1, n_x)
        ]

    def column(value):
        return jnp.sum(value, axis=0, keepdims=True)

    def sums_start(k, terms):
        which_row = lax.broadcasted_iota(jnp.int32, (8, tile), 0)
        packed = jnp.zeros((8, tile), F32)
        for i, term in enumerate(terms):
            packed = jnp.where(which_row == i, term, packed)
        red_y[k, my_y] = packed
        for copy in sum_y(k):
            copy.start()

    def sums_middle(k):
        for copy in sum_y(k):
            copy.wait_recv()
        red_x[k, my_x] = jnp.sum(red_y[k], axis=0)
        for copy in sum_x(k):
            copy.start()

    def sums_end(k):
        for copy in sum_x(k):
            copy.wait_recv()
        totals = jnp.sum(jnp.sum(red_x[k], axis=0), axis=1, keepdims=True)
        return [totals[i : i + 1, :] for i in range(8)]

    residual = right_ref[...]
    image = operate(0, residual)
    r_ref[...] = residual
    w_now[...] = image
    sums_start(0, (column(residual * residual), column(residual * image)))
    s_now[...] = image
    nearby[1, 4] = (live[...] * image).astype(BF16)
    for copy in halo(1):
        copy.start()
    onward[...] = operate(1, image, lambda: sums_middle(0))
    norm_now, product = sums_end(0)[:2]
    alpha = norm_now / product
    x_ref[...] = alpha * residual
    d_now[...] = residual
    residual = residual - alpha * s_now[...]
    image = image - alpha * onward[...]
    for k in range(1, ITERS - 1):
        final = k + 2 == ITERS
        r_ref[...] = residual
        w_now[...] = image
        sums_start(k, (column(residual * residual), column(residual * image)))
        nearby[k + 1, 4] = (live[...] * image).astype(BF16)
        for copy in halo(k + 1):
            copy.start()
        coefficients = []

        def advance():
            norm_next, product = sums_end(k)[:2]
            ratio = norm_next / norm_now
            alpha_next = norm_next / (product - ratio * norm_next / alpha)
            coefficients.extend((norm_next, ratio, alpha_next))
            d_now[...] = r_ref[...] + ratio * d_now[...]
            s_now[...] = w_now[...] + ratio * s_now[...]
            x_ref[...] += alpha_next * d_now[...]
            r_ref[...] -= alpha_next * s_now[...]

        def early(energy):
            advance()
            r_next, w, q = r_ref[...], w_now[...], onward[...]
            sums_start(
                k + 1,
                (column(r_next * r_next), column(r_next * w), column(r_next * q), column(w * w), column(q * w), energy),
            )

        if final:
            further = operate(k + 1, image, lambda: sums_middle(k), early)
        else:
            further = operate(k + 1, image, lambda: sums_middle(k))
            advance()
        norm_now, ratio, alpha = coefficients
        onward[...] = further + ratio * onward[...]
        residual = r_ref[...]
        image = w_now[...] - alpha * onward[...]
    norm_last, r_w, r_q, w_w, q_w, energy = sums_end(ITERS - 1)[:6]
    product = r_w - alpha * (w_w - alpha * (energy + ratio * q_w)) - alpha * ratio * r_q
    ratio = norm_last / norm_now
    alpha = norm_last / (product - ratio * norm_last / alpha)
    x_ref[...] += alpha * (residual + ratio * d_now[...])
    r_ref[...] = residual - alpha * (image + ratio * s_now[...])

    for k in range(ITERS):
        for copy in halo(k) + relay(k, 1) + relay(k, -1) + returns(k) + sum_y(k) + sum_x(k):
            copy.wait_send()
    for copy in degrees_y() + degrees_x():
        copy.wait_send()


def hand_over(x_in, r_in, x_out, r_out):
    x_out[...] = x_in[...]
    r_out[...] = r_in[...]


def on_device(mesh_sizes, right_side, compress, block_fill, pair_home, pair_far, pair_count, weights):
    n_x, n_y = mesh_sizes
    blocks, tile = right_side.shape
    npairs = weights.shape[0]
    chunks = 4
    dma = pltpu.SemaphoreType.DMA
    vmem = pl.BlockSpec(memory_space=pltpu.VMEM)
    out = jax.ShapeDtypeStruct((blocks, tile), F32)
    x, r = pl.pallas_call(
        functools.partial(kernel, (n_x, n_y, chunks)),
        out_shape=(out, out),
        in_specs=[pl.BlockSpec(memory_space=pl.ANY)] * 5
        + [pl.BlockSpec(memory_space=pltpu.SMEM), pl.BlockSpec(memory_space=pl.ANY)],
        out_specs=(vmem, vmem),
        scratch_shapes=[
            pltpu.VMEM((blocks, tile), F32),
            pltpu.VMEM((blocks, tile), F32),
            pltpu.VMEM((1, blocks), jnp.int32),
            pltpu.VMEM((1, npairs), jnp.int32),
            pltpu.VMEM((1, npairs), jnp.int32),
            pltpu.VMEM((npairs, tile, tile), BF16),
            pltpu.VMEM((npairs, tile, tile), BF16),
            pltpu.VMEM((blocks, npairs), BF16),
            pltpu.VMEM((npairs, blocks), BF16),
            pltpu.VMEM((9 * blocks, npairs), BF16),
            pltpu.VMEM((npairs, 9 * blocks), BF16),
            pltpu.VMEM((GROUP, GROUP * tile), BF16),
            pltpu.VMEM((blocks, tile), F32),
            pltpu.VMEM((blocks, tile), F32),
            pltpu.VMEM((npairs, tile), BF16),
            pltpu.VMEM((npairs, tile), BF16),
            pltpu.VMEM((npairs, tile), F32),
            pltpu.VMEM((blocks, tile), F32),
            pltpu.VMEM((blocks, tile), F32),
            pltpu.VMEM((blocks, tile), F32),
            pltpu.VMEM((blocks, tile), F32),
            pltpu.VMEM((blocks, tile), F32),
            pltpu.VMEM((ITERS, 9, blocks, tile), BF16),
            pltpu.VMEM((ITERS, 9, blocks, tile), BF16),
            pltpu.VMEM((ITERS, 9, blocks, tile), BF16),
            pltpu.VMEM((9, blocks, tile), F32),
            pltpu.VMEM((9, blocks, tile), BF16),
            pltpu.VMEM((9, blocks, tile), BF16),
            pltpu.VMEM((ITERS, n_y, 8, tile), F32),
            pltpu.VMEM((ITERS, n_x, 8, tile), F32),
            dma((chunks,)),
            dma((5,)),
            dma((ITERS, 9)),
            dma((ITERS, 9)),
            dma((ITERS, 9)),
            dma((ITERS, 9)),
            dma((9,)),
            dma((9,)),
            dma((ITERS, n_y)),
            dma((ITERS, n_y)),
            dma((ITERS, n_x)),
            dma((ITERS, n_x)),
        ],
        compiler_params=pltpu.CompilerParams(
            collective_id=0, has_side_effects=True, vmem_limit_bytes=56 * 1024 * 1024
        ),
    )(right_side, compress, block_fill, pair_home, pair_far, pair_count, weights)
    return pl.pallas_call(hand_over, out_shape=(out, out), in_specs=[vmem] * 2, out_specs=(vmem, vmem))(x, r)


def solution(mesh):
    return jax.shard_map(
        functools.partial(on_device, (mesh.shape["gx"], mesh.shape["gy"])),
        mesh=mesh,
        in_specs=(
            P(("gx", "gy"), None),
            P(("gx", "gy"), None),
            P(("gx", "gy")),
            P(("gx", "gy")),
            P(("gx", "gy")),
            P(("gx", "gy")),
            P(("gx", "gy"), None, None),
        ),
        out_specs=(P(("gx", "gy"), None), P(("gx", "gy"), None)),
        check_vma=False,
    )
```
